32 devices in a mesh: dp: 16 (over z, y, x), tensor: 2 (over core).
Axes of the slice: x: 2, y: 2, z: 4, core: 2. Of those that a mesh axis runs over, the one named last changes fastest.
Arguments:
- inputs: bfloat16 [6144, 2560], P(('dp', 'tensor')), may hold values from -6 to 6
- gain_one: float32 [2560], replicated, may hold values from 0.5 to 1.5
- w_x: bfloat16 [2560, 2560], P('dp', 'tensor'), may hold values from -0.125 to 0.125
- w_y: bfloat16 [2560, 2560], P('dp', 'tensor'), may hold values from -0.125 to 0.125
- conv_w: float32 [4, 2560], replicated, may hold values from -3 to 3
- gate_a: bfloat16 [10, 256, 256], P('tensor', 'dp'), may hold values from -0.375 to 0.375
- gate_i: bfloat16 [10, 256, 256], P('tensor', 'dp'), may hold values from -0.375 to 0.375
- decay: float32 [2560], replicated, may hold values from -9 to -1
- w_out: bfloat16 [2560, 2560], P('dp', 'tensor'), may hold values from -0.3125 to 0.3125
- gain_two: float32 [2560], replicated, may hold values from 0.5 to 1.5
- w_gate: bfloat16 [2560, 7680], P('dp', 'tensor'), may hold values from -0.125 to 0.125
- w_up: bfloat16 [2560, 7680], P('dp', 'tensor'), may hold values from -0.125 to 0.125
- w_down: bfloat16 [2560, 7680], P('dp', 'tensor'), may hold values from -0.125 to 0.125
- segment_ids: int32 [6144], replicated, may hold values from 0 to 1, never falling along the last dimension, each value on 1 to 4096 neighbouring positions
- cotangent: bfloat16 [6144, 2560], P(('dp', 'tensor')), may hold values from -6 to 6
Outputs:
- block_out: bfloat16 [6144, 2560], P(('dp', 'tensor'))
- grad_inputs: float32 [6144, 2560], P(('dp', 'tensor'))
- grad_gain_one: float32 [2560], replicated
- grad_w_x: float32 [2560, 2560], P('dp', 'tensor')
- grad_w_y: float32 [2560, 2560], P('dp', 'tensor')
- grad_conv: float32 [4, 2560], replicated
- grad_gate_a: float32 [10, 256, 256], P('tensor', 'dp')
- grad_gate_i: float32 [10, 256, 256], P('tensor', 'dp')
- grad_decay: float32 [2560], replicated
- grad_w_out: float32 [2560, 2560], P('dp', 'tensor')
- grad_gain_two: float32 [2560], replicated
- grad_w_gate: float32 [2560, 7680], P('dp', 'tensor')
- grad_w_up: float32 [2560, 7680], P('dp', 'tensor')
- grad_w_down: float32 [2560, 7680], P('dp', 'tensor')
The draws below stay inside these ranges and needn't reach their ends.
Inputs may be any that keep to these rules, and one draw needn't show every extreme that they name: `segment_ids`: segment numbers never fall along the tokens; each segment holds 1 to 4096 tokens.
All inputs are finite; a program needn't handle non-finite values.
Results may differ from the reference program's by a relative error of at most 0.02.
Values may be sent and summed in bfloat16 or wider, within the bound.
No kernel may reach another device: no remote copies, remote signals or barrier semaphores. Data moves between devices by JAX's collectives and lax.ppermute only.
A program may use at most 384 MiB of HBM per device.

```python
import math
import jax
import jax.numpy as jnp
import numpy as np
from jax import lax

D = 2560
FF = 7680
H = 10
HW = 256
CONV = 4
TOKENS = 6144
SEQS = 2
MOST = 4096


def block_scale(rng, extent, shards, low, largest):
    factor_of = 1.0
    for dim, parts in shards:
        draws = jax.random.uniform(jax.random.fold_in(jax.random.fold_in(rng, 6), dim), (parts,), jnp.float32, low / len(shards), largest / len(shards))
        factor_of = factor_of * jnp.repeat(jnp.exp(draws), extent[dim] // parts).reshape((-1,) + (1,) * (len(extent) - 1 - dim))
    return factor_of


def split_up(count, total, reach, skew):
    portions = [(1 << 20) // math.isqrt(rank ** skew) + 1 for rank in range(2, count + 1)]
    spare, holding = total - reach - (count - 1), [1] * (count - 1)
    while spare > 0:
        free = [i for i in range(count - 1) if holding[i] < reach]
        pool, left = sum([portions[i] for i in free]), spare
        for i in free:
            addition = min(reach - holding[i], max(1, left * portions[i] // pool), spare)
            holding[i] = holding[i] + addition
            spare = spare - addition
    return np.array([reach] + holding)


def ragged(own_key, amount, total, bound, lean):
    if amount == 2:
        one = jax.random.randint(own_key, (), max(1, total - bound), min(bound, total - 1) + 1)
        return jnp.stack([one, total - one])
    sizes = jnp.asarray(split_up(amount, total, bound, lean), jnp.int32)
    pairs = (amount - 1) // 2
    giver, taker = sizes[1:1 + 2 * pairs:2], sizes[2:2 + 2 * pairs:2]
    slack = jnp.minimum(giver - 1, bound - taker)
    shifted = jax.random.randint(jax.random.fold_in(own_key, 1), (pairs,), 0, 1 << 20) % (slack + 1)
    sizes = sizes.at[1:1 + 2 * pairs:2].set(giver - shifted).at[2:2 + 2 * pairs:2].set(taker + shifted)
    return sizes[jax.random.permutation(jax.random.fold_in(own_key, 2), amount)]


def scatter_about(own_key, extent, spread, most, cuts=(), kind=jnp.bfloat16):
    entries = jax.random.normal(own_key, extent, jnp.float32) * spread
    if len(cuts) > 0:
        entries = block_scale(own_key, extent, cuts, -0.22, 0.18) * entries
    return jnp.clip(entries, min=-most, max=most).astype(kind)


def setup_inputs(seed: int = 0) -> dict:
    seeds = jax.random.split(jax.random.key(seed), 16)
    inputs = scatter_about(seeds[0], (TOKENS, D), 1.0, 6.0, ((0, 32),))
    gain_one = jnp.clip(1.0 + 0.1 * jax.random.normal(seeds[1], (D,), jnp.float32), 0.5, 1.5)
    w_x = scatter_about(seeds[2], (D, D), D ** -0.5, 0.125, ((0, 16), (1, 2)))
    w_y = scatter_about(seeds[3], (D, D), D ** -0.5, 0.125, ((0, 16), (1, 2)))
    conv_w = scatter_about(seeds[4], (CONV, D), CONV ** -0.5, 3.0, (), jnp.float32)
    gate_a = scatter_about(seeds[5], (H, HW, HW), HW ** -0.5, 0.375, ((0, 2), (1, 16)))
    gate_i = scatter_about(seeds[6], (H, HW, HW), HW ** -0.5, 0.375, ((0, 2), (1, 16)))
    decay = jnp.clip(jax.random.uniform(seeds[7], (D,), jnp.float32, -9.0, -1.0), -9.0, -1.0)
    w_out = scatter_about(seeds[8], (D, D), (D // 8) ** -0.5, 0.3125, ((0, 16), (1, 2)))
    gain_two = jnp.clip(1.0 + 0.1 * jax.random.normal(seeds[9], (D,), jnp.float32), 0.5, 1.5)
    w_gate = scatter_about(seeds[10], (D, FF), D ** -0.5, 0.125, ((0, 16), (1, 2)))
    w_up = scatter_about(seeds[11], (D, FF), D ** -0.5, 0.125, ((0, 16), (1, 2)))
    w_down = scatter_about(seeds[12], (D, FF), (FF // 4) ** -0.5, 0.125, ((0, 16), (1, 2)))
    segment_ids = jnp.searchsorted(jnp.cumsum(ragged(seeds[13], SEQS, TOKENS, MOST, 1)), jnp.arange(TOKENS), side="right").astype(jnp.int32)
    cotangent = scatter_about(seeds[14], (TOKENS, D), 1.0, 6.0, ((0, 32),))
    return {"inputs": inputs, "gain_one": gain_one, "w_x": w_x, "w_y": w_y, "conv_w": conv_w, "gate_a": gate_a, "gate_i": gate_i, "decay": decay, "w_out": w_out, "gain_two": gain_two, "w_gate": w_gate, "w_up": w_up, "w_down": w_down, "segment_ids": segment_ids, "cotangent": cotangent}


EPS = 1e-06

@jax.custom_vjp
def low(v):
    return lax.optimization_barrier(v.astype(jnp.bfloat16)).astype(jnp.float32)

@jax.custom_vjp
def low_back(v):
    return v

def low_keep(v):
    return (low(v), None)

def low_pass(kept, grad):
    return (grad,)

def back_keep(v):
    return (v, None)

def back_low(kept, grad):
    return (low(grad),)
low.defvjp(low_keep, low_pass)
low_back.defvjp(back_keep, back_low)

def gelu_tanh(values):
    return jax.nn.gelu(values, approximate=True)

def matmul(left, right):
    return jnp.dot(left, right, precision=lax.Precision.HIGHEST)

def matmul_nt(left, right):
    return lax.dot_general(left, right, (((1,), (1,)), ((), ())), precision=lax.Precision.HIGHEST)

def rms_unit(values):
    return values * lax.rsqrt(lax.optimization_barrier(jnp.mean(values * values, axis=-1, keepdims=True)) + EPS)

def compose(earlier, later):
    return (earlier[0] * later[0], later[0] * earlier[1] + later[1])

def forward(inputs, gain_one, w_x, w_y, conv_w, gate_a, gate_i, decay, w_out, gain_two, w_gate, w_up, w_down, segment_ids):
    count = inputs.shape[0]
    padded_ids = jnp.concatenate([jnp.full((3,), -1, jnp.int32), segment_ids.astype(jnp.int32)])
    own_ids = padded_ids[3:]
    start = (own_ids != padded_ids[2:2 + count]).astype(jnp.float32)[:, None]
    carry_on = 1.0 - start
    normed1 = low(rms_unit(inputs) * gain_one)
    x_branch = low(low_back(matmul(normed1, w_x)))
    y_pre = low_back(matmul(normed1, w_y))
    y_act = gelu_tanh(y_pre)
    conv = jnp.zeros_like(x_branch)
    for shift_by in range(4):
        earlier_rows = jnp.concatenate([jnp.zeros((shift_by, x_branch.shape[1]), jnp.float32), x_branch[:count - shift_by]], axis=0)
        same = (own_ids == padded_ids[3 - shift_by:3 - shift_by + count]).astype(jnp.float32)[:, None]
        conv = conv + conv_w[shift_by] * earlier_rows * same
    conv_low = low(low_back(conv))
    heads = conv_low.reshape(count, H, HW)
    gate_pre_a = low_back(jnp.einsum('thi,hij->thj', heads, gate_a, precision=lax.Precision.HIGHEST).reshape(count, D))
    gate_pre_i = low_back(jnp.einsum('thi,hij->thj', heads, gate_i, precision=lax.Precision.HIGHEST).reshape(count, D))
    rate = jax.nn.sigmoid(gate_pre_a)
    inflow = jax.nn.sigmoid(gate_pre_i)
    log_decay = -8.0 * jax.nn.softplus(decay) * rate
    factor = jnp.exp(log_decay) * carry_on
    mult = carry_on * jnp.sqrt(-jnp.expm1(2.0 * log_decay)) + start
    drive = mult * inflow * conv_low
    _, state = lax.associative_scan(compose, (factor, drive), axis=0)
    mixed = low(low_back(state * y_act))
    branch = low_back(matmul_nt(mixed, w_out))
    middle = inputs + branch
    normed2 = low(rms_unit(middle) * gain_two)
    gate_pre = low_back(matmul(normed2, w_gate))
    up_pre = low_back(matmul(normed2, w_up))
    hidden = low(gelu_tanh(gate_pre) * up_pre)
    return middle + low_back(matmul_nt(hidden, w_down))

def reference(inputs, gain_one, w_x, w_y, conv_w, gate_a, gate_i, decay, w_out, gain_two, w_gate, w_up, w_down, segment_ids, cotangent):
    floats = tuple((weight_in.astype(jnp.float32) for weight_in in (inputs, gain_one, w_x, w_y, conv_w, gate_a, gate_i, decay, w_out, gain_two, w_gate, w_up, w_down)))

    def apply_block(*params):
        return forward(*params, segment_ids)
    result, pullback = jax.vjp(apply_block, *floats)
    grads = pullback(cotangent.astype(jnp.float32))
    return (result.astype(jnp.bfloat16), grads[0], grads[1], grads[2], grads[3], grads[4], grads[5], grads[6], grads[7], grads[8], grads[9], grads[10], grads[11], grads[12])
```

```python
import functools
import math
import jax
import jax.numpy as jnp
from jax import lax
from jax.experimental import pallas as pl
from jax.experimental.pallas import tpu as pltpu
from jax.sharding import Mesh, PartitionSpec as P

EPS = 1e-06
LOW = jnp.bfloat16
FULL = jnp.float32
PLANE = ("y", "x")
DP = ("z", "y", "x")
GELU_ROOT = math.sqrt(2.0 / math.pi)
SWAP = [(0, 1), (1, 0)]


def gelu_tanh(values):
    return jax.nn.gelu(values, approximate=True)


def matmul(left, right):
    return jnp.dot(left, right, preferred_element_type=FULL)


def matmul_nt(left, right):
    return lax.dot_general(left, right, (((1,), (1,)), ((), ())), preferred_element_type=FULL)


def matmul_tn(left, right):
    return lax.dot_general(left, right, (((0,), (0,)), ((), ())), preferred_element_type=FULL)


def pick(array, index):
    return lax.dynamic_index_in_dim(array, index, 0, keepdims=False)


def put(array, part, index):
    return lax.dynamic_update_index_in_dim(array, part, index, 0)


def swap_core(array):
    return lax.ppermute(array, "c", SWAP)


def to_mate(array, mate):
    if mate == 1:
        return lax.ppermute(array, "x", SWAP)
    if mate == 2:
        return lax.ppermute(array, "y", SWAP)
    return lax.ppermute(array, PLANE, [(i, 3 - i) for i in range(4)])


def turn(array, by):
    depth = lax.axis_size("z")
    return lax.ppermute(array, "z", [(i, (i + by) % depth) for i in range(depth)])


def exchange_plane(blocks, mine):
    got = blocks
    for mate in (1, 2, 3):
        got = put(got, to_mate(pick(blocks, mine ^ mate), mate), mine ^ mate)
    return got


def exchange_depth(blocks, mine):
    depth = blocks.shape[0]
    got = blocks
    for by in range(1, depth):
        part = turn(pick(blocks, (mine + by) % depth), by)
        got = put(got, part, (mine - by) % depth)
    return got


def gather_plane(array, mine):
    got = put(jnp.zeros((4,) + array.shape, array.dtype), array, mine)
    for mate in (1, 2, 3):
        got = put(got, to_mate(array, mate), mine ^ mate)
    return got


def gather_depth(array, mine, depth):
    got = put(jnp.zeros((depth,) + array.shape, array.dtype), array, mine)
    for by in range(1, depth):
        got = put(got, turn(array, by), (mine - by) % depth)
    return got


def both_cores(array, core):
    other = swap_core(array)
    got = jnp.zeros((array.shape[0], 2) + array.shape[1:], array.dtype)
    got = lax.dynamic_update_slice_in_dim(got, array[:, None], core, 1)
    return lax.dynamic_update_slice_in_dim(got, other[:, None], 1 - core, 1)


def own_core(array, core):
    away = lax.dynamic_index_in_dim(array, 1 - core, 1, keepdims=False)
    home = lax.dynamic_index_in_dim(array, core, 1, keepdims=False)
    return home.astype(FULL) + swap_core(away).astype(FULL)


def sum_depth(array, mine):
    depth = array.shape[0]
    low = array.astype(LOW)
    total = pick(array, mine)
    for by in range(1, depth):
        total = total + turn(pick(low, (mine + by) % depth), by).astype(FULL)
    return total


def sum_all(array):
    for axis in DP:
        size, reach = lax.axis_size(axis), 1
        while reach < size:
            array = array + lax.ppermute(array, axis, [(i, i ^ reach) for i in range(size)])
            reach *= 2
    return array


def col_blocks(array, count):
    width = array.shape[1] // count
    main = width // 128 * 128
    rest = width - main
    parts = []
    for i in range(count):
        piece = array[:, i * main : (i + 1) * main]
        if rest:
            start = count * main + i * rest
            piece = jnp.concatenate([piece, array[:, start : start + rest]], axis=1)
        parts.append(piece)
    return jnp.stack(parts)


def col_join(blocks):
    count, _, width = blocks.shape
    main = width // 128 * 128
    parts = [blocks[i][:, :main] for i in range(count)]
    if main < width:
        parts += [blocks[i][:, main:] for i in range(count)]
    return jnp.concatenate(parts, axis=1)


def permute_kernel(order, width, in_ref, out_ref):
    for to, come in enumerate(order):
        out_ref[:, to * width : (to + 1) * width] = in_ref[:, come * width : (come + 1) * width].astype(
            out_ref.dtype
        )


def permute_columns(array, order, dtype):
    rows, columns = array.shape
    return pl.pallas_call(
        functools.partial(permute_kernel, tuple(order), columns // len(order)),
        out_shape=jax.ShapeDtypeStruct((rows, columns), dtype),
    )(array)


def minus_expm1(value):
    series = 1.0 + value * (1.0 / 7.0)
    for n in (6.0, 5.0, 4.0, 3.0, 2.0):
        series = 1.0 + value * (1.0 / n) * series
    return jnp.where(value > -0.35, -value * series, 1.0 - jnp.exp(value))


def dot_tn(left, right):
    return lax.dot_general(left, right, (((0,), (0,)), ((), ())), preferred_element_type=FULL)


def gelu_parts(v):
    t = jnp.tanh(GELU_ROOT * (v + 0.044715 * v * v * v))
    act = 0.5 * v * (1.0 + t)
    slope = 0.5 * (1.0 + t) + 0.5 * v * (1.0 - t * t) * GELU_ROOT * (1.0 + 3.0 * 0.044715 * v * v)
    return act, slope


def scan_tiles(factor_ref, drive_ref, sums_ref, runs_ref, backward):
    rows, columns = factor_ref.shape
    place = lax.broadcasted_iota(jnp.int32, (8, columns), 0)

    def tile(step, carry):
        run, total = carry
        at = pl.multiple_of((rows // 8 - 1 - step if backward else step) * 8, 8)
        f = factor_ref[pl.ds(at, 8), :]
        d = drive_ref[pl.ds(at, 8), :]
        for reach in (1, 2, 4):
            turn_by = 8 - reach if backward else reach
            inside = place < 8 - reach if backward else place >= reach
            f_near = jnp.where(inside, pltpu.roll(f, turn_by, 0), 1.0)
            d_near = jnp.where(inside, pltpu.roll(d, turn_by, 0), 0.0)
            d = d + f * d_near
            f = f * f_near
        d = d + f * total
        f = f * run
        sums_ref[pl.ds(at, 8), :] = d
        runs_ref[pl.ds(at, 8), :] = f
        edge = 0 if backward else 7
        return f[edge : edge + 1, :], d[edge : edge + 1, :]

    start = (jnp.ones((1, columns), FULL), jnp.zeros((1, columns), FULL))
    return lax.fori_loop(0, rows // 8, tile, start, unroll=2)


def forward_kernel(
    x_ref, tail_ref, mask_ref, taps_ref, soft_ref, ga_ref, gi_ref,
    conv_ref, rate_ref, inflow_ref, sums_ref, runs_ref, ends_ref,
    pad_ref, factor_ref, drive_ref,
):
    rows = x_ref.shape[0]
    pad_ref[0:8, :] = tail_ref[...].astype(FULL)
    pad_ref[8 : rows + 8, :] = x_ref[...].astype(FULL)
    conv = taps_ref[0:1, :] * pad_ref[8 : rows + 8, :]
    for k in (1, 2, 3):
        conv = conv + taps_ref[k : k + 1, :] * pad_ref[8 - k : rows + 8 - k, :] * mask_ref[:, k - 1 : k]
    conv_low = conv.astype(LOW)
    conv_ref[...] = conv_low
    rate = jax.nn.sigmoid(jnp.dot(conv_low, ga_ref[...], preferred_element_type=FULL))
    inflow = jax.nn.sigmoid(jnp.dot(conv_low, gi_ref[...], preferred_element_type=FULL))
    rate_ref[...] = rate
    inflow_ref[...] = inflow
    start = mask_ref[:, 3:4]
    keep = 1.0 - start
    log_decay = -8.0 * soft_ref[0:1, :] * rate
    root = jnp.sqrt(minus_expm1(2.0 * log_decay))
    factor_ref[...] = jnp.exp(log_decay) * keep
    drive_ref[...] = (keep * root + start) * inflow * conv_low.astype(FULL)
    run, total = scan_tiles(factor_ref, drive_ref, sums_ref, runs_ref, False)
    ends_ref[0:1, :] = run
    ends_ref[1:2, :] = total


def adjoint_kernel(
    dmix_ref, y_ref, state_ref, rate_ref, mask_ref, soft_ref,
    sums_ref, runs_ref, dy_ref, ends_ref,
    pad_ref, ahead_ref, drive_ref,
):
    rows = y_ref.shape[0]
    act, slope = gelu_parts(y_ref[...].astype(FULL))
    dmix = dmix_ref[...].astype(FULL)
    dy_ref[...] = (dmix * state_ref[...] * slope).astype(LOW)
    drive_ref[...] = dmix * act
    factor = jnp.exp(-8.0 * soft_ref[0:1, :] * rate_ref[...]) * (1.0 - mask_ref[:, 3:4])
    pad_ref[0:rows, :] = factor
    pad_ref[rows : rows + 8, :] = jnp.ones((8, factor.shape[1]), FULL)
    ahead_ref[...] = pad_ref[1 : rows + 1, :]
    run, total = scan_tiles(ahead_ref, drive_ref, sums_ref, runs_ref, True)
    ends_ref[0:1, :] = pad_ref[0:1, :] * run
    ends_ref[1:2, :] = pad_ref[0:1, :] * total


def gates_back_kernel(
    sums_ref, runs_ref, inbound_ref, state_ref, rate_ref, inflow_ref, conv_ref, x_ref, tail_ref,
    mask_ref, soft_ref, ga_ref, gi_ref,
    dconv_ref, gga_ref, ggi_ref, small_ref,
    pad_ref,
):
    rows = x_ref.shape[0]
    start = mask_ref[:, 3:4]
    keep = 1.0 - start
    soft = soft_ref[0:1, :]
    conv_low = conv_ref[...]
    conv = conv_low.astype(FULL)
    rate = rate_ref[...]
    inflow = inflow_ref[...]
    log_decay = -8.0 * soft * rate
    decay_now = jnp.exp(log_decay)
    root = jnp.sqrt(minus_expm1(2.0 * log_decay))
    mult = keep * root + start
    adjoint = sums_ref[...] + runs_ref[...] * inbound_ref[1:2, :]
    pad_ref[0:8, :] = jnp.broadcast_to(inbound_ref[0:1, :], (8, conv.shape[1]))
    pad_ref[8 : rows + 8, :] = state_ref[...]
    before = pad_ref[7 : rows + 7, :]
    d_mult = adjoint * inflow * conv
    d_inflow = adjoint * mult * conv
    d_log = keep * (adjoint * before * decay_now - d_mult * decay_now * decay_now / root)
    small_ref[4:5, :] = jnp.sum(d_log * (-8.0 * rate), axis=0, keepdims=True)
    d_rate = (d_log * (-8.0 * soft) * rate * (1.0 - rate)).astype(LOW)
    d_in = (d_inflow * inflow * (1.0 - inflow)).astype(LOW)
    gga_ref[...] = dot_tn(conv_low, d_rate).astype(gga_ref.dtype)
    ggi_ref[...] = dot_tn(conv_low, d_in).astype(ggi_ref.dtype)
    d_conv = adjoint * mult * inflow + matmul_nt(d_rate, ga_ref[...]) + matmul_nt(d_in, gi_ref[...])
    low = d_conv.astype(LOW)
    dconv_ref[...] = low
    d_conv = low.astype(FULL)
    pad_ref[0:8, :] = tail_ref[...].astype(FULL)
    pad_ref[8 : rows + 8, :] = x_ref[...].astype(FULL)
    small_ref[0:1, :] = jnp.sum(d_conv * pad_ref[8 : rows + 8, :], axis=0, keepdims=True)
    for k in (1, 2, 3):
        product = d_conv * pad_ref[8 - k : rows + 8 - k, :] * mask_ref[:, k - 1 : k]
        small_ref[k : k + 1, :] = jnp.sum(product, axis=0, keepdims=True)


def conv_back_kernel(dconv_ref, lead_ref, mask_ref, taps_ref, dx_ref, pad_ref):
    rows = dconv_ref.shape[0]
    pad_ref[0:rows, :] = dconv_ref[...].astype(FULL)
    pad_ref[rows : rows + 8, :] = lead_ref[...].astype(FULL)
    total = taps_ref[0:1, :] * pad_ref[0:rows, :]
    for k in (1, 2, 3):
        total = total + taps_ref[k : k + 1, :] * pad_ref[k : rows + k, :] * mask_ref[:, k + 3 : k + 4]
    dx_ref[...] = total.astype(LOW)


def by_head(kernel, heads, ins, outs, scratch):
    rows_of = {"full": lambda a: pl.BlockSpec((a.shape[0], a.shape[1] // heads), lambda h: (0, h)),
               "gate": lambda a: pl.BlockSpec((None,) + a.shape[1:], lambda h: (h, 0, 0)),
               "same": lambda a: pl.BlockSpec(a.shape, lambda h: (0, 0))}
    return pl.pallas_call(
        kernel,
        grid=(heads,),
        in_specs=[rows_of[kind](a) for kind, a in ins],
        out_specs=[rows_of[kind](a) for kind, a in outs],
        out_shape=[a for _, a in outs],
        scratch_shapes=scratch,
    )(*[a for _, a in ins])


def join(earlier, later):
    return jnp.stack([earlier[0] * later[0], later[0] * earlier[1] + later[1]])


def carried_in(ends, q, z, depth, backward):
    none = jnp.stack([jnp.ones_like(ends[0]), jnp.zeros_like(ends[0])])
    parts = gather_plane(ends, q)
    before, plane = none, none
    for j in range(3, -1, -1) if backward else range(4):
        part = parts[j]
        inside = j > q if backward else j < q
        before = jnp.where(inside, join(before, part), before)
        plane = join(plane, part)
    far = none
    for by in range(depth - 1, 0, -1):
        if backward:
            got = lax.ppermute(plane, "z", [(i + by, i) for i in range(depth - by)])
            there = z + by < depth
        else:
            got = lax.ppermute(plane, "z", [(i, i + by) for i in range(depth - by)])
            there = z >= by
        far = jnp.where(there, join(far, got), far)
    return join(far, before)[1]


def norm_forward(values):
    scale = lax.rsqrt(jnp.mean(values * values, axis=-1, keepdims=True) + EPS)
    return values * scale, scale


def norm_backward(unit, scale, gain, upstream):
    weighted = upstream * gain
    inner = jnp.mean(weighted * unit, axis=-1, keepdims=True)
    return scale * (weighted - unit * inner), jnp.sum(upstream * unit, axis=0)


def rec_blocks(wx, wy):
    xb, yb = col_blocks(wx, 4), col_blocks(wy, 4)
    main = xb.shape[2] // 128 * 128
    return jnp.concatenate([xb[:, :, :main], yb[:, :, :main], xb[:, :, main:], yb[:, :, main:]], axis=2)


def rec_split(slab):
    n = slab.shape[2] // 2
    main = n // 128 * 128
    rest = n - main
    first = [slab[j][:, :main] for j in range(4)] + [slab[j][:, 2 * main : 2 * main + rest] for j in range(4)]
    second = [slab[j][:, main : 2 * main] for j in range(4)] + [slab[j][:, 2 * main + rest :] for j in range(4)]
    return jnp.concatenate(first, axis=1), jnp.concatenate(second, axis=1)


def on_device(
    inputs, gain_one, w_x, w_y, conv_w, gate_a, gate_i, decay, w_out, gain_two,
    w_gate, w_up, w_down, segment_ids, cotangent,
):
    depth = lax.axis_size("z")
    z, core = lax.axis_index("z"), lax.axis_index("c")
    q = lax.axis_index(PLANE)
    block = 4 * z + q
    share, width = inputs.shape
    rows = w_x.shape[0]
    chan = w_x.shape[1]
    heads, gate_rows, head_width = gate_a.shape
    toks = 2 * share
    count = depth * 4
    into = [zz * 4 + qq for qq in range(4) for zz in range(depth)]
    back = [qq * depth + zz for zz in range(depth) for qq in range(4)]

    def turned(vector):
        return vector.reshape(depth, 4, rows).transpose(1, 0, 2).reshape(width)

    def unturned(vector):
        return vector.reshape(4, depth, rows).transpose(1, 0, 2).reshape(width)

    first = block * toks
    padded = jnp.concatenate([jnp.full((3,), -1, jnp.int32), segment_ids, jnp.full((3,), -2, jnp.int32)])
    near = lax.dynamic_slice_in_dim(padded, first, toks + 6)
    own = near[3 : 3 + toks]
    marks = [own == near[3 - k : 3 - k + toks] for k in (1, 2, 3)]
    marks.append(own != near[2 : 2 + toks])
    marks += [own == near[3 + k : 3 + k + toks] for k in (1, 2, 3)]
    marks.append(own == own)
    mask = jnp.stack(marks, axis=1).astype(FULL)
    taps = lax.dynamic_slice_in_dim(conv_w, core * chan, chan, 1)
    decay_part = lax.dynamic_slice_in_dim(decay, core * chan, chan, 0)
    soft = jax.nn.softplus(decay_part)[None, :]
    gain1, gain2 = turned(gain_one), turned(gain_two)

    source = permute_columns(inputs, into, LOW).astype(FULL)
    unit1, scale1 = norm_forward(source)
    normed1 = (unit1 * gain1).astype(LOW)
    slab = exchange_plane(rec_blocks(w_x, w_y), q)
    w_xy = lax.all_gather(slab, "z", axis=1, tiled=True).reshape(width, -1)
    mates = [normed1] + [to_mate(normed1, mate) for mate in (1, 2, 3)]
    full1 = both_cores(jnp.stack(mates), core).reshape(4 * toks, width)

    gates = jnp.stack([gate_a, gate_i]).reshape(-1, head_width)
    gates = gather_depth(gather_plane(gates, q), z, depth)
    gates = gates.reshape(depth, 4, 2, heads, gate_rows, head_width).transpose(2, 3, 0, 1, 4, 5)
    gates = gates.reshape(2, heads, head_width, head_width)

    w_out_z = lax.all_gather(w_out, "z", axis=0, tiled=True)
    w_out_full = gather_plane(w_out_z, q).reshape(width, chan)

    def fetch(weight):
        mine = exchange_depth(col_blocks(weight, depth), z)
        return lax.all_gather(mine.reshape(depth * rows, -1), PLANE, axis=0, tiled=True)

    wg, wu = fetch(w_gate), fetch(w_up)
    wd = fetch(w_down)

    projected = matmul(full1, w_xy).astype(LOW).reshape(4, toks, -1)
    pieces = jnp.zeros_like(projected)
    for mate in range(4):
        part = projected[mate] if mate == 0 else to_mate(projected[mate], mate)
        pieces = put(pieces, part, q ^ mate)
    x_branch, y_pre = rec_split(pieces)
    order = [(i, i + 1) for i in range(count - 1)]
    tail = lax.ppermute(x_branch[toks - 8 :], DP, order)
    shape_of = jax.ShapeDtypeStruct
    wide = shape_of((toks, chan), FULL)
    thin = shape_of((toks, chan), LOW)
    conv_low, rate, inflow, sums, runs, ends = by_head(
        forward_kernel, heads,
        [("full", x_branch), ("full", tail), ("same", mask), ("full", taps), ("full", soft),
         ("gate", gates[0]), ("gate", gates[1])],
        [("full", thin)] + [("full", wide)] * 4 + [("full", shape_of((2, chan), FULL))],
        [pltpu.VMEM((toks + 8, head_width), FULL)] + [pltpu.VMEM((toks, head_width), FULL)] * 2,
    )
    inbound = carried_in(ends, q, z, depth, False)
    state = sums + runs * inbound
    mixed = (state * gelu_tanh(y_pre.astype(FULL))).astype(LOW)
    branch = matmul_nt(mixed, w_out_full).astype(LOW).reshape(1, 2, share, width)
    middle = source + own_core(branch, core)[0]
    unit2, scale2 = norm_forward(middle)
    normed2 = (unit2 * gain2).astype(LOW)

    back_in = permute_columns(cotangent, into, LOW)
    full_g = both_cores(gather_depth(back_in, z, depth), core).reshape(depth * toks, width)
    full2 = both_cores(gather_depth(normed2, z, depth), core).reshape(depth * toks, width)
    gate_pre = matmul(full2, wg)
    up_pre = matmul(full2, wu)
    activated, gate_pull = jax.vjp(gelu_tanh, gate_pre)
    hidden = (activated * up_pre).astype(LOW)
    d_hidden = matmul(full_g, wd)
    d_gate = gate_pull(d_hidden * up_pre)[0].astype(LOW)
    d_up = (d_hidden * activated).astype(LOW)

    def home(partial):
        halves = own_core(partial.astype(LOW).reshape(depth, 2, share, width), core)
        return sum_depth(halves, z)

    d_normed2 = home(matmul_nt(d_gate, wg) + matmul_nt(d_up, wu))
    out_low = (middle + home(matmul_nt(hidden, wd))).astype(LOW)
    block_out = permute_columns(out_low, back, LOW)

    def return_weight(grad):
        mine = lax.psum_scatter(grad.astype(LOW), PLANE, scatter_dimension=0, tiled=True)
        return col_join(exchange_depth(mine.reshape(depth, rows, -1), z)).astype(FULL)

    grad_down = return_weight(matmul_tn(full_g, hidden))
    grad_gate = return_weight(matmul_tn(full2, d_gate))
    grad_up = return_weight(matmul_tn(full2, d_up))

    d_norm, grad_gain_two = norm_backward(unit2, scale2, gain2, d_normed2)
    d_middle = back_in.astype(FULL) + d_norm
    full_branch = both_cores(d_middle.astype(LOW)[None], core).reshape(toks, width)

    d_mixed = matmul(full_branch, w_out_full).astype(LOW)
    grad_out = matmul_tn(full_branch, mixed).astype(LOW)
    back_sums, back_runs, d_y, back_ends = by_head(
        adjoint_kernel, heads,
        [("full", d_mixed), ("full", y_pre), ("full", state), ("full", rate), ("same", mask), ("full", soft)],
        [("full", wide), ("full", wide), ("full", thin), ("full", shape_of((2, chan), FULL))],
        [pltpu.VMEM((toks + 8, head_width), FULL)] + [pltpu.VMEM((toks, head_width), FULL)] * 2,
    )
    coming = carried_in(back_ends, q, z, depth, True)
    carries = jnp.stack([inbound, coming])
    square = shape_of((heads, head_width, head_width), LOW)
    d_conv, gga, ggi, small = by_head(
        gates_back_kernel, heads,
        [("full", back_sums), ("full", back_runs), ("full", carries), ("full", state), ("full", rate),
         ("full", inflow), ("full", conv_low), ("full", x_branch), ("full", tail), ("same", mask),
         ("full", soft), ("gate", gates[0]), ("gate", gates[1])],
        [("full", thin), ("gate", square), ("gate", square), ("full", shape_of((5, chan), FULL))],
        [pltpu.VMEM((toks + 8, head_width), FULL)],
    )
    lead = lax.ppermute(d_conv[:8], DP, [(j, i) for i, j in order])
    (d_x,) = by_head(
        conv_back_kernel, heads,
        [("full", d_conv), ("full", lead), ("same", mask), ("full", taps)],
        [("full", thin)],
        [pltpu.VMEM((toks + 8, head_width), FULL)],
    )
    d_slab = rec_blocks(d_x, d_y)
    d_parts = [pick(d_slab, q)] + [to_mate(pick(d_slab, q ^ mate), mate) for mate in (1, 2, 3)]
    d_xy = jnp.stack(d_parts).reshape(4 * toks, -1)
    d_full1 = matmul_nt(d_xy, w_xy).astype(LOW).reshape(4, 2, share, width)
    halves1 = own_core(d_full1, core)
    low1 = halves1.astype(LOW)
    d_normed1 = halves1[0]
    for mate in (1, 2, 3):
        d_normed1 = d_normed1 + to_mate(low1[mate], mate).astype(FULL)

    grad_xy = matmul_tn(full1, d_xy).astype(LOW).reshape(4, depth * rows, -1)
    grad_xy = lax.psum_scatter(grad_xy, "z", scatter_dimension=1, tiled=True)
    grad_wx, grad_wy = rec_split(exchange_plane(grad_xy, q))

    gate_grads = jnp.stack([gga, ggi]).reshape(2, heads, depth, 4, gate_rows, head_width)
    gate_grads = gate_grads.transpose(3, 2, 0, 1, 4, 5).reshape(4, depth * rows, head_width)
    out_slab = jnp.concatenate([grad_out.reshape(4, depth * rows, chan), gate_grads], axis=2)
    out_sum = pick(out_slab, q).astype(FULL)
    for mate in (1, 2, 3):
        out_sum = out_sum + to_mate(pick(out_slab, q ^ mate), mate).astype(FULL)
    out_own = lax.psum_scatter(out_sum.astype(LOW), "z", scatter_dimension=0, tiled=True).astype(FULL)
    grad_w_out = out_own[:, :chan]
    gate_own = out_own[:, chan:].reshape(2, heads, gate_rows, head_width)

    d_input_norm, grad_gain_one = norm_backward(unit1, scale1, gain1, d_normed1)
    grad_inputs = permute_columns(d_middle + d_input_norm, back, FULL)

    decay_row = (small[4] * jax.nn.sigmoid(decay_part))[None]
    gains = jnp.stack([grad_gain_one, grad_gain_two]).reshape(4, chan)
    gains = gains + swap_core(gains)
    packed = sum_all(jnp.concatenate([gains, small[:4], decay_row], axis=0))
    mine = packed[4:]
    other = swap_core(mine)
    low_half = jnp.where(core == 0, mine, other)
    high_half = jnp.where(core == 0, other, mine)
    small_full = jnp.concatenate([low_half, high_half], axis=1)
    gain_sums = packed[:4].reshape(2, width)
    return (
        block_out,
        grad_inputs,
        unturned(gain_sums[0]),
        grad_wx.astype(FULL),
        grad_wy.astype(FULL),
        small_full[:4],
        gate_own[0],
        gate_own[1],
        small_full[4],
        grad_w_out,
        unturned(gain_sums[1]),
        grad_gate,
        grad_up,
        grad_down,
    )


def solution(mesh):
    depth = mesh.shape["dp"] // 4
    fine = Mesh(mesh.devices.reshape(depth, 2, 2, 2), ("z", "y", "x", "c"))
    tokens = P(("z", "y", "x", "c"), None)
    weight = P(DP, "c")
    gate = P("c", DP, None)
    placed = (
        tokens, P(), weight, weight, P(), gate, gate, P(), weight, P(),
        weight, weight, weight, P(), tokens,
    )
    return jax.shard_map(
        on_device,
        mesh=fine,
        in_specs=placed,
        out_specs=(
            tokens, tokens, P(), weight, weight, P(), gate, gate, P(), weight, P(),
            weight, weight, weight,
        ),
        check_vma=False,
    )
```
